1024 devices in a mesh: dp: 128 (over z, x_hi, core), zero: 8 (over y, x_lo).
Axes of the slice: x: 4 (x_hi: 2, x_lo: 2; x = x_hi * 2 + x_lo), y: 4, z: 32, core: 2. Of those that a mesh axis runs over, the one named last changes fastest.
Arguments:
- pre_acts: bfloat16 [131072, 2560], P(('dp', 'zero')), may hold values from -6 to 6
- cotangent: bfloat16 [131072, 640], P(('dp', 'zero')), may hold values from -24 to 24
- w_out: bfloat16 [1280, 640], P('zero'), may hold values from -0.25 to 0.25
Outputs:
- d_pre: bfloat16 [131072, 2560], P(('dp', 'zero'))
- d_w: float32 [8, 102400], P('zero', 'dp')
The draws below stay inside these ranges and needn't reach their ends.
All inputs are finite; a program needn't handle non-finite values.
Results may differ from the reference program's by a relative error of at most 0.0028.
Values may be sent and summed in bfloat16 or wider, within the bound.
No kernel may reach another device: no remote copies, remote signals or barrier semaphores. Data moves between devices by JAX's collectives and lax.ppermute only.
A program may use at most 32 MiB of HBM per device.

```python
import math
import jax
import jax.numpy as jnp
from jax import lax

D = 640
FFH = 1280
TOKENS = 131072
N_ZERO = 8


def strengthened(array, own_key, source, target, blocks, factor):
    owner, partner = [(jnp.arange(array.shape[dim]) // (array.shape[dim] // blocks)).reshape([-1 if axis == dim else 1 for axis in range(array.ndim)]) for dim in (source, target)]
    chosen = jax.random.permutation(own_key, blocks)[partner]
    strong = (owner == chosen) | (owner == (partner + blocks // 2) % blocks)
    return jnp.where(strong, factor * array, array)


def block_scale(stream_key, dims, shards, least, largest):
    level = 1.0
    for position, blocks in shards:
        draws = jax.random.uniform(jax.random.fold_in(jax.random.fold_in(stream_key, 6), position), (blocks,), jnp.float32, least / len(shards), largest / len(shards))
        level = level * jnp.repeat(jnp.exp(draws), dims[position] // blocks).reshape((-1,) + (1,) * (len(dims) - 1 - position))
    return level


def scatter_about(key, dims, scale, most, cuts=(), dtype=jnp.bfloat16):
    drawn = jax.random.normal(key, dims, jnp.float32) * scale
    if len(cuts) > 0:
        drawn = block_scale(key, dims, cuts, -0.22, 0.18) * drawn
    return jnp.clip(drawn, min=-most, max=most).astype(dtype)


def bell_draw_with(stream_key, extent, width, reach, split, heavy, dtype=jnp.bfloat16):
    drawn = width * jax.random.normal(stream_key, extent, jnp.float32)
    if split:
        drawn = drawn * block_scale(stream_key, extent, split, -0.22, 0.18)
    return jnp.clip(strengthened(drawn, jax.random.fold_in(stream_key, 3), *heavy), -reach, reach).astype(dtype)


def setup_inputs(seed: int = 0) -> dict:
    seeds = jax.random.split(jax.random.key(seed), 4)
    return {
        "pre_acts": scatter_about(seeds[0], (TOKENS, 2 * FFH), 1.0, 6.0, ((0, 1024),)),
        "cotangent": bell_draw_with(seeds[1], (TOKENS, D), 1.0, 24.0, ((0, 1024),), (0, 1, 128, 5.5)),
        "w_out": scatter_about(seeds[2], (FFH, D), D ** -0.5, 0.25, ((0, 8),)),
    }


def block_grads(pre_acts, cotangent, w_out):
    value = pre_acts[:, :FFH].astype(jnp.float32)
    gate = pre_acts[:, FFH:].astype(jnp.float32)
    cdf = 0.5 * (1.0 + jax.scipy.special.erf(gate / math.sqrt(2.0)))
    act = gate * cdf
    hidden = (value * act).astype(jnp.bfloat16)
    term = jnp.dot(hidden.T, cotangent, preferred_element_type=jnp.float32)
    d_hidden = jnp.dot(cotangent, w_out.T, preferred_element_type=jnp.float32)
    dens = jnp.exp(-0.5 * gate * gate) / math.sqrt(2.0 * math.pi)
    d_value = d_hidden * act
    d_gate = d_hidden * value * (cdf + gate * dens)
    d_pre = jnp.concatenate([d_value, d_gate], axis=1).astype(jnp.bfloat16)
    return (d_pre, term)

def reference(pre_acts, cotangent, w_out):
    block = min(TOKENS, 4096)
    count = TOKENS // block
    pre_blocks = pre_acts.reshape(count, block, 2 * FFH)
    cot_blocks = cotangent.reshape(count, block, D)

    def step(carry, items):
        d_pre, term = block_grads(items[0], items[1], w_out)
        return (carry + term, d_pre)
    start = jnp.zeros((FFH, D), jnp.float32)
    total, outs = lax.scan(step, start, (pre_blocks, cot_blocks))
    d_w = (total / math.sqrt(TOKENS)).reshape(N_ZERO, FFH * D // N_ZERO)
    return (outs.reshape(TOKENS, 2 * FFH), d_w)
```

```python
import math

import jax
import jax.numpy as jnp
from jax import lax
from jax.experimental import pallas as pl
from jax.experimental.pallas import tpu as pltpu
from jax.sharding import Mesh, PartitionSpec as P


D = 640
FFH = 1280
OWN = 160
GROUP = 8
TOK = 128
LANES = 128
COLS = D // LANES
FAR = 32
NEAR = 4
PIECE = 800
ROWS = 8
GROUP_AXES = ("y", "xl")
NEAR_AXES = ("xh", "c")
FAR_AXES = ("z",)
DP_AXES = FAR_AXES + NEAR_AXES
VMEM = pl.BlockSpec(memory_space=pltpu.VMEM)
SMEM = pl.BlockSpec(memory_space=pltpu.SMEM)


def cdf_of(gate):
    return 0.5 * (1.0 + lax.erf(gate * (1.0 / math.sqrt(2.0))))


def outgoing_kernel(pre_ref, cot_ref, out_ref, ht_ref):
    for c in range(COLS):
        block = cot_ref[:, pl.ds(c * LANES, LANES)]
        for s in range(GROUP):
            out_ref[s, pl.ds(c * TOK, TOK), :] = block
    for j in range(FFH // LANES):
        cols = pl.ds(j * LANES, LANES)
        value = pre_ref[:, cols].astype(jnp.float32)
        gate = pre_ref[:, pl.ds(FFH + j * LANES, LANES)].astype(jnp.float32)
        hidden = value * (gate * cdf_of(gate))
        ht_ref[cols, :] = hidden.T.astype(jnp.bfloat16)
    for s in range(GROUP):
        out_ref[s, pl.ds(D, OWN), :] = ht_ref[pl.ds(s * OWN, OWN), :]


def factors_kernel(pre_ref, act_ref, slope_ref):
    for j in range(FFH // LANES):
        cols = pl.ds(j * LANES, LANES)
        value = pre_ref[:, cols].astype(jnp.float32)
        gate = pre_ref[:, pl.ds(FFH + j * LANES, LANES)].astype(jnp.float32)
        cdf = cdf_of(gate)
        dens = jnp.exp(-0.5 * gate * gate) * (1.0 / math.sqrt(2.0 * math.pi))
        act_ref[:, cols] = gate * cdf
        slope_ref[:, cols] = value * (cdf + gate * dens)


def products_kernel(scale, near_ref, in_ref, w_ref, dh_ref, own_ref, *refs):
    outs, flat_ref, parts_ref = refs[: NEAR - 1], refs[-2], refs[-1]
    cots = jnp.concatenate(
        [
            jnp.concatenate([in_ref[s, pl.ds(c * TOK, TOK), :] for c in range(COLS)], axis=1)
            for s in range(GROUP)
        ],
        axis=0,
    )
    dht = lax.dot_general(w_ref[...], cots, (((1,), (1,)), ((), ())), preferred_element_type=jnp.float32)
    for s in range(GROUP):
        dh_ref[s] = dht[:, s * TOK : (s + 1) * TOK]
    ht = jnp.concatenate([in_ref[s, pl.ds(D, OWN), :] for s in range(GROUP)], axis=1)
    total = jnp.dot(ht, cots, preferred_element_type=jnp.float32) * scale
    for c in range(COLS):
        flat_ref[pl.ds(c, OWN, stride=COLS), :] = total[:, c * LANES : (c + 1) * LANES]
    flat_ref[pl.ds(OWN * COLS, ROWS), :] = jnp.zeros((ROWS, LANES), jnp.float32)
    for far in range(FAR):
        for near in range(NEAR):
            first = (far * NEAR + near) * PIECE // LANES
            parts_ref[near, far] = flat_ref[pl.ds(first, ROWS), :]
    mine = near_ref[0]
    own_ref[...] = parts_ref[mine]
    for j in range(1, NEAR):
        outs[j - 1][...] = parts_ref[jnp.bitwise_xor(mine, j)].astype(jnp.bfloat16)


def near_sum_kernel(own_ref, *refs):
    total = own_ref[...]
    for ref in refs[:-1]:
        total += ref[...].astype(jnp.float32)
    refs[-1][...] = total.astype(jnp.bfloat16)


def d_pre_kernel(dh_ref, act_ref, slope_ref, out_ref):
    for j in range(FFH // LANES):
        cols = pl.ds(j * LANES, LANES)
        dh = dh_ref[cols, :].T
        out_ref[:, cols] = (dh * act_ref[:, cols]).astype(jnp.bfloat16)
        out_ref[:, pl.ds(FFH + j * LANES, LANES)] = (dh * slope_ref[:, cols]).astype(jnp.bfloat16)


def far_sum_kernel(near_ref, got_ref, out_ref, line_ref):
    total = jnp.zeros((ROWS, LANES), jnp.float32)
    for far in range(FAR):
        total += got_ref[far].astype(jnp.float32)
    for row in range(ROWS):
        line_ref[:, pl.ds(row * LANES, LANES)] = total[row : row + 1, :]
    for near in range(NEAR):

        @pl.when(near_ref[0] == near)
        def _():
            out_ref[...] = line_ref[:, pl.ds(near * PIECE % LANES, PIECE)]


def call(kernel, out, *args, flops=0, scratch=()):
    outs = out if isinstance(out, tuple) else (out,)
    moved = sum(a.size * a.dtype.itemsize for a in args) + sum(o.size * o.dtype.itemsize for o in outs)
    return pl.pallas_call(
        kernel,
        out_shape=out,
        in_specs=[SMEM if a.dtype == jnp.int32 else VMEM for a in args],
        out_specs=(VMEM,) * len(outs) if isinstance(out, tuple) else VMEM,
        compiler_params=pltpu.CompilerParams(vmem_limit_bytes=16 << 20),
        cost_estimate=pl.CostEstimate(flops=flops, bytes_accessed=moved, transcendentals=0),
        scratch_shapes=list(scratch),
    )(*args)


def body(pre_acts, cotangent, w_out):
    scale = 1.0 / math.sqrt(TOK * GROUP * NEAR * FAR)
    bf16, f32 = jnp.bfloat16, jnp.float32
    S = jax.ShapeDtypeStruct
    near = (lax.axis_index("xh") * 2 + lax.axis_index("c")).astype(jnp.int32).reshape(1)

    outgoing = call(
        outgoing_kernel, S((GROUP, D + OWN, TOK), bf16), pre_acts, cotangent,
        scratch=[pltpu.VMEM((FFH, TOK), bf16)],
    )
    incoming = lax.all_to_all(outgoing, GROUP_AXES, 0, 0)
    block = (FAR, ROWS, LANES)
    dh, own, *parts = call(
        lambda *refs: products_kernel(scale, *refs),
        (S((GROUP, OWN, TOK), f32), S(block, f32)) + (S(block, bf16),) * (NEAR - 1),
        near, incoming, w_out,
        flops=4 * OWN * D * TOK * GROUP,
        scratch=[pltpu.VMEM((OWN * COLS + ROWS, LANES), f32), pltpu.VMEM((NEAR,) + block, f32)],
    )
    dh = lax.all_to_all(dh, GROUP_AXES, 0, 0)
    parts = [lax.ppermute(part, NEAR_AXES, [(i, i ^ (j + 1)) for i in range(NEAR)]) for j, part in enumerate(parts)]
    summed = call(near_sum_kernel, S(block, bf16), own, *parts)
    got = lax.all_to_all(summed, FAR_AXES, 0, 0)
    act, slope = call(factors_kernel, (S((TOK, FFH), f32),) * 2, pre_acts)
    d_pre = call(d_pre_kernel, S((TOK, 2 * FFH), bf16), dh.reshape(FFH, TOK), act, slope)
    d_w = call(
        far_sum_kernel, S((1, PIECE), f32), near, got, scratch=[pltpu.VMEM((1, ROWS * LANES), f32)]
    )
    return (d_pre, d_w)


def solution(mesh):
    fine = Mesh(mesh.devices.reshape(FAR, 2, 2, 4, 2), DP_AXES + GROUP_AXES)
    return jax.shard_map(
        body,
        mesh=fine,
        in_specs=(P(DP_AXES + GROUP_AXES, None), P(DP_AXES + GROUP_AXES, None), P(GROUP_AXES, None)),
        out_specs=(P(DP_AXES + GROUP_AXES, None), P(GROUP_AXES, DP_AXES)),
        check_vma=False,
    )
```

```python
import math

import jax
import jax.numpy as jnp
from jax import lax
from jax.experimental import pallas as pl
from jax.experimental.pallas import tpu as pltpu
from jax.sharding import Mesh, PartitionSpec as P


D = 640
FFH = 1280
OWN = 160
GROUP = 8
TOK = 128
LANES = 128
COLS = D // LANES
FAR = 32
NEAR = 4
PIECE = 800
ROWS = 8
GROUP_AXES = ("y", "xl")
NEAR_AXES = ("xh", "c")
FAR_AXES = ("z",)
FAR_ORDER = [(i + 16) % FAR for i in range(FAR)]
DP_AXES = FAR_AXES + NEAR_AXES
VMEM = pl.BlockSpec(memory_space=pltpu.VMEM)
SMEM = pl.BlockSpec(memory_space=pltpu.SMEM)


def cdf_of(gate):
    return 0.5 * (1.0 + lax.erf(gate * (1.0 / math.sqrt(2.0))))


def outgoing_kernel(_, pre_ref, cot_ref, out_ref, ht_ref):
    for c in range(COLS):
        block = cot_ref[:, pl.ds(c * LANES, LANES)]
        for s in range(GROUP):
            out_ref[s, pl.ds(c * TOK, TOK), :] = block
    for j in range(FFH // LANES):
        cols = pl.ds(j * LANES, LANES)
        value = pre_ref[:, cols].astype(jnp.float32)
        gate = pre_ref[:, pl.ds(FFH + j * LANES, LANES)].astype(jnp.float32)
        hidden = value * (gate * cdf_of(gate))
        ht_ref[cols, :] = hidden.T.astype(jnp.bfloat16)
    for s in range(GROUP):
        out_ref[s, pl.ds(D, OWN), :] = ht_ref[pl.ds(s * OWN, OWN), :]


def factors_kernel(pre_ref, act_ref, slope_ref):
    for j in range(FFH // LANES):
        cols = pl.ds(j * LANES, LANES)
        value = pre_ref[:, cols].astype(jnp.float32)
        gate = pre_ref[:, pl.ds(FFH + j * LANES, LANES)].astype(jnp.float32)
        cdf = cdf_of(gate)
        dens = jnp.exp(-0.5 * gate * gate) * (1.0 / math.sqrt(2.0 * math.pi))
        act_ref[:, cols] = gate * cdf
        slope_ref[:, cols] = value * (cdf + gate * dens)


def products_kernel(scale, near_ref, in_ref, w_ref, dh_ref, own_ref, *refs):
    outs, flat_ref, parts_ref = refs[: NEAR - 1], refs[-2], refs[-1]
    cots = jnp.concatenate(
        [
            jnp.concatenate([in_ref[s, pl.ds(c * TOK, TOK), :] for c in range(COLS)], axis=1)
            for s in range(GROUP)
        ],
        axis=0,
    )
    dht = lax.dot_general(w_ref[...], cots, (((1,), (1,)), ((), ())), preferred_element_type=jnp.float32)
    for s in range(GROUP):
        dh_ref[s] = dht[:, s * TOK : (s + 1) * TOK]
    ht = jnp.concatenate([in_ref[s, pl.ds(D, OWN), :] for s in range(GROUP)], axis=1)
    total = jnp.dot(ht, cots, preferred_element_type=jnp.float32) * scale
    for c in range(COLS):
        flat_ref[pl.ds(c, OWN, stride=COLS), :] = total[:, c * LANES : (c + 1) * LANES]
    flat_ref[pl.ds(OWN * COLS, ROWS), :] = jnp.zeros((ROWS, LANES), jnp.float32)
    for far in range(FAR):
        for near in range(NEAR):
            first = (far * NEAR + near) * PIECE // LANES
            parts_ref[near, FAR_ORDER.index(far)] = flat_ref[pl.ds(first, ROWS), :]
    mine = near_ref[0]
    own_ref[...] = parts_ref[mine]
    for j in range(1, NEAR):
        outs[j - 1][...] = parts_ref[jnp.bitwise_xor(mine, j)].astype(jnp.bfloat16)


def near_sum_kernel(_, own_ref, *refs):
    total = own_ref[...]
    for ref in refs[:-1]:
        total += ref[...].astype(jnp.float32)
    refs[-1][...] = total.astype(jnp.bfloat16)


def d_pre_kernel(dh_ref, act_ref, slope_ref, out_ref, done_ref):
    done_ref[...] = jnp.zeros_like(done_ref)
    for j in range(FFH // LANES):
        cols = pl.ds(j * LANES, LANES)
        dh = dh_ref[cols, :].T
        out_ref[:, cols] = (dh * act_ref[:, cols]).astype(jnp.bfloat16)
        out_ref[:, pl.ds(FFH + j * LANES, LANES)] = (dh * slope_ref[:, cols]).astype(jnp.bfloat16)


def far_sum_kernel(near_ref, got_ref, out_ref, line_ref):
    total = jnp.zeros((ROWS, LANES), jnp.float32)
    for far in range(FAR):
        total += got_ref[far].astype(jnp.float32)
    for row in range(ROWS):
        line_ref[:, pl.ds(row * LANES, LANES)] = total[row : row + 1, :]
    for near in range(NEAR):

        @pl.when(near_ref[0] == near)
        def _():
            out_ref[...] = line_ref[:, pl.ds(near * PIECE % LANES, PIECE)]


def call(kernel, out, *args, flops=0, scratch=()):
    outs = out if isinstance(out, tuple) else (out,)
    moved = sum(a.size * a.dtype.itemsize for a in args) + sum(o.size * o.dtype.itemsize for o in outs)
    return pl.pallas_call(
        kernel,
        out_shape=out,
        in_specs=[SMEM if a.dtype == jnp.int32 else VMEM for a in args],
        out_specs=(VMEM,) * len(outs) if isinstance(out, tuple) else VMEM,
        compiler_params=pltpu.CompilerParams(vmem_limit_bytes=16 << 20),
        cost_estimate=pl.CostEstimate(flops=flops, bytes_accessed=moved, transcendentals=0),
        scratch_shapes=list(scratch),
    )(*args)


def body(pre_acts, cotangent, w_out):
    scale = 1.0 / math.sqrt(TOK * GROUP * NEAR * FAR)
    bf16, f32 = jnp.bfloat16, jnp.float32
    S = jax.ShapeDtypeStruct
    near = (lax.axis_index("xh") * 2 + lax.axis_index("c")).astype(jnp.int32).reshape(1)

    outgoing = call(
        outgoing_kernel, S((GROUP, D + OWN, TOK), bf16), near, pre_acts, cotangent,
        scratch=[pltpu.VMEM((FFH, TOK), bf16)],
    )
    incoming = lax.all_to_all(outgoing, GROUP_AXES, 0, 0)
    block = (FAR, ROWS, LANES)
    dh, own, *parts = call(
        lambda *refs: products_kernel(scale, *refs),
        (S((GROUP, OWN, TOK), f32), S(block, f32)) + (S(block, bf16),) * (NEAR - 1),
        near, incoming, w_out,
        flops=4 * OWN * D * TOK * GROUP,
        scratch=[pltpu.VMEM((OWN * COLS + ROWS, LANES), f32), pltpu.VMEM((NEAR,) + block, f32)],
    )
    dh = lax.all_to_all(dh, GROUP_AXES, 0, 0)
    parts = [lax.ppermute(part, NEAR_AXES, [(i, i ^ (j + 1)) for i in range(NEAR)]) for j, part in enumerate(parts)]
    act, slope = call(factors_kernel, (S((TOK, FFH), f32),) * 2, pre_acts)
    d_pre, done = call(d_pre_kernel, (S((TOK, 2 * FFH), bf16), S((ROWS, LANES), f32)), dh.reshape(FFH, TOK), act, slope)
    summed = call(near_sum_kernel, S(block, bf16), done, own, *parts)
    got = lax.all_to_all(summed, "z", 0, 0, axis_index_groups=[FAR_ORDER])
    d_w = call(
        far_sum_kernel, S((1, PIECE), f32), near, got, scratch=[pltpu.VMEM((1, ROWS * LANES), f32)]
    )
    return (d_pre, d_w)


def solution(mesh):
    fine = Mesh(mesh.devices.reshape(FAR, 2, 2, 4, 2), DP_AXES + GROUP_AXES)
    return jax.shard_map(
        body,
        mesh=fine,
        in_specs=(P(DP_AXES + GROUP_AXES, None), P(DP_AXES + GROUP_AXES, None), P(GROUP_AXES, None)),
        out_specs=(P(DP_AXES + GROUP_AXES, None), P(GROUP_AXES, DP_AXES)),
        check_vma=False,
    )
```

```python
import math

import jax
import jax.numpy as jnp
from jax import lax
from jax.experimental import pallas as pl
from jax.experimental.pallas import tpu as pltpu
from jax.sharding import Mesh, PartitionSpec as P


D = 640
FFH = 1280
OWN = 160
GROUP = 8
TOK = 128
LANES = 128
COLS = D // LANES
FAR = 32
NEAR = 4
PIECE = 800
ROWS = 8
GROUP_AXES = ("y", "xl")
NEAR_AXES = ("xh", "c")
FAR_AXES = ("z",)
FAR_ORDER = [(i + 16) % FAR for i in range(FAR)]
DP_AXES = FAR_AXES + NEAR_AXES
VMEM = pl.BlockSpec(memory_space=pltpu.VMEM)
SMEM = pl.BlockSpec(memory_space=pltpu.SMEM)


def cdf_of(gate):
    return 0.5 * (1.0 + lax.erf(gate * (1.0 / math.sqrt(2.0))))


def outgoing_kernel(_, pre_ref, cot_ref, out_ref, ht_ref):
    for c in range(COLS):
        block = cot_ref[:, pl.ds(c * LANES, LANES)]
        for s in range(GROUP):
            out_ref[s, pl.ds(c * TOK, TOK), :] = block
    for j in range(FFH // LANES):
        cols = pl.ds(j * LANES, LANES)
        value = pre_ref[:, cols].astype(jnp.float32)
        gate = pre_ref[:, pl.ds(FFH + j * LANES, LANES)].astype(jnp.float32)
        hidden = value * (gate * cdf_of(gate))
        ht_ref[cols, :] = hidden.T.astype(jnp.bfloat16)
    for s in range(GROUP):
        out_ref[s, pl.ds(D, OWN), :] = ht_ref[pl.ds(s * OWN, OWN), :]


def factors_kernel(pre_ref, act_ref, slope_ref):
    for j in range(FFH // LANES):
        cols = pl.ds(j * LANES, LANES)
        value = pre_ref[:, cols].astype(jnp.float32)
        gate = pre_ref[:, pl.ds(FFH + j * LANES, LANES)].astype(jnp.float32)
        cdf = cdf_of(gate)
        dens = jnp.exp(-0.5 * gate * gate) * (1.0 / math.sqrt(2.0 * math.pi))
        act_ref[:, cols] = gate * cdf
        slope_ref[:, cols] = value * (cdf + gate * dens)


def products_kernel(scale, at_ref, in_ref, w_ref, dh_ref, keep_ref, give_ref, flat_ref, parts_ref):
    cots = jnp.concatenate(
        [
            jnp.concatenate([in_ref[s, pl.ds(c * TOK, TOK), :] for c in range(COLS)], axis=1)
            for s in range(GROUP)
        ],
        axis=0,
    )
    dht = lax.dot_general(w_ref[...], cots, (((1,), (1,)), ((), ())), preferred_element_type=jnp.float32)
    for s in range(GROUP):
        dh_ref[s] = dht[:, s * TOK : (s + 1) * TOK]
    ht = jnp.concatenate([in_ref[s, pl.ds(D, OWN), :] for s in range(GROUP)], axis=1)
    total = jnp.dot(ht, cots, preferred_element_type=jnp.float32) * scale
    for c in range(COLS):
        flat_ref[pl.ds(c, OWN, stride=COLS), :] = total[:, c * LANES : (c + 1) * LANES]
    flat_ref[pl.ds(OWN * COLS, ROWS), :] = jnp.zeros((ROWS, LANES), jnp.float32)
    for far in range(FAR):
        for near in range(NEAR):
            first = (far * NEAR + near) * PIECE // LANES
            parts_ref[near, FAR_ORDER.index(far)] = flat_ref[pl.ds(first, ROWS), :]
    core = lax.rem(at_ref[0], 2)
    for half in range(2):
        keep_ref[half] = parts_ref[half * 2 + core]
        give_ref[half] = parts_ref[half * 2 + 1 - core]


def core_sum_kernel(at_ref, own_ref, got_ref, keep_ref, give_ref):
    half = lax.div(at_ref[0], 2)
    keep_ref[...] = own_ref[half] + got_ref[half]
    give_ref[...] = (own_ref[1 - half] + got_ref[1 - half]).astype(jnp.bfloat16)


def near_sum_kernel(_, own_ref, got_ref, out_ref):
    out_ref[...] = (own_ref[...] + got_ref[...].astype(jnp.float32)).astype(jnp.bfloat16)


def d_pre_kernel(dh_ref, act_ref, slope_ref, out_ref, done_ref):
    done_ref[...] = jnp.zeros_like(done_ref)
    for j in range(FFH // LANES):
        cols = pl.ds(j * LANES, LANES)
        dh = dh_ref[cols, :].T
        out_ref[:, cols] = (dh * act_ref[:, cols]).astype(jnp.bfloat16)
        out_ref[:, pl.ds(FFH + j * LANES, LANES)] = (dh * slope_ref[:, cols]).astype(jnp.bfloat16)


def far_sum_kernel(at_ref, got_ref, out_ref, line_ref):
    total = jnp.zeros((ROWS, LANES), jnp.float32)
    for far in range(FAR):
        total += got_ref[far].astype(jnp.float32)
    for row in range(ROWS):
        line_ref[:, pl.ds(row * LANES, LANES)] = total[row : row + 1, :]
    for near in range(NEAR):

        @pl.when(at_ref[0] == near)
        def _():
            out_ref[...] = line_ref[:, pl.ds(near * PIECE % LANES, PIECE)]


def call(kernel, out, *args, flops=0, scratch=()):
    outs = out if isinstance(out, tuple) else (out,)
    moved = sum(a.size * a.dtype.itemsize for a in args) + sum(o.size * o.dtype.itemsize for o in outs)
    return pl.pallas_call(
        kernel,
        out_shape=out,
        in_specs=[SMEM if a.dtype == jnp.int32 else VMEM for a in args],
        out_specs=(VMEM,) * len(outs) if isinstance(out, tuple) else VMEM,
        compiler_params=pltpu.CompilerParams(vmem_limit_bytes=16 << 20),
        cost_estimate=pl.CostEstimate(flops=flops, bytes_accessed=moved, transcendentals=0),
        scratch_shapes=list(scratch),
    )(*args)


def body(pre_acts, cotangent, w_out):
    scale = 1.0 / math.sqrt(TOK * GROUP * NEAR * FAR)
    bf16, f32 = jnp.bfloat16, jnp.float32
    S = jax.ShapeDtypeStruct
    at = (lax.axis_index("xh") * 2 + lax.axis_index("c")).astype(jnp.int32).reshape(1)

    outgoing = call(
        outgoing_kernel, S((GROUP, D + OWN, TOK), bf16), at, pre_acts, cotangent,
        scratch=[pltpu.VMEM((FFH, TOK), bf16)],
    )
    incoming = lax.all_to_all(outgoing, GROUP_AXES, 0, 0)
    block = (FAR, ROWS, LANES)
    dh, keep, give = call(
        lambda *refs: products_kernel(scale, *refs),
        (S((GROUP, OWN, TOK), f32), S((2,) + block, f32), S((2,) + block, f32)),
        at, incoming, w_out,
        flops=4 * OWN * D * TOK * GROUP,
        scratch=[pltpu.VMEM((OWN * COLS + ROWS, LANES), f32), pltpu.VMEM((NEAR,) + block, f32)],
    )
    dh = lax.all_to_all(dh, GROUP_AXES, 0, 0)
    got = lax.ppermute(give, "c", [(0, 1), (1, 0)])
    keep, give = call(core_sum_kernel, (S(block, f32), S(block, bf16)), at, keep, got)
    got = lax.ppermute(give, "xh", [(0, 1), (1, 0)])
    act, slope = call(factors_kernel, (S((TOK, FFH), f32),) * 2, pre_acts)
    d_pre, done = call(d_pre_kernel, (S((TOK, 2 * FFH), bf16), S((ROWS, LANES), f32)), dh.reshape(FFH, TOK), act, slope)
    summed = call(near_sum_kernel, S(block, bf16), done, keep, got)
    got = lax.all_to_all(summed, "z", 0, 0, axis_index_groups=[FAR_ORDER])
    d_w = call(
        far_sum_kernel, S((1, PIECE), f32), at, got, scratch=[pltpu.VMEM((1, ROWS * LANES), f32)]
    )
    return (d_pre, d_w)


def solution(mesh):
    fine = Mesh(mesh.devices.reshape(FAR, 2, 2, 4, 2), DP_AXES + GROUP_AXES)
    return jax.shard_map(
        body,
        mesh=fine,
        in_specs=(P(DP_AXES + GROUP_AXES, None), P(DP_AXES + GROUP_AXES, None), P(GROUP_AXES, None)),
        out_specs=(P(DP_AXES + GROUP_AXES, None), P(GROUP_AXES, DP_AXES)),
        check_vma=False,
    )
```

```python
import math

import jax
import jax.numpy as jnp
from jax import lax
from jax.experimental import pallas as pl
from jax.experimental.pallas import tpu as pltpu
from jax.sharding import Mesh, PartitionSpec as P


D = 640
FFH = 1280
OWN = 160
GROUP = 8
TOK = 128
LANES = 128
COLS = D // LANES
FAR = 32
NEAR = 4
PIECE = 800
ROWS = 8
GROUP_AXES = ("y", "xl")
NEAR_AXES = ("xh", "c")
FAR_AXES = ("z",)
GROUP_ORDER = [5, 4, 7, 6, 1, 0, 3, 2]
FAR_ORDER = [(i + 16) % FAR for i in range(FAR)]
DP_AXES = FAR_AXES + NEAR_AXES
VMEM = pl.BlockSpec(memory_space=pltpu.VMEM)
ANY = pl.BlockSpec(memory_space=pl.ANY)
SMEM = pl.BlockSpec(memory_space=pltpu.SMEM)


def cdf_of(gate):
    return 0.5 * (1.0 + lax.erf(gate * (1.0 / math.sqrt(2.0))))


def outgoing_kernel(_, pre_hbm, cot_hbm, out_hbm, pre_ref, cot_ref, cols_ref, ht_ref, in_sems, out_sems):
    cot_copy = pltpu.make_async_copy(cot_hbm, cot_ref, in_sems.at[0])
    cot_copy.start()
    pre_copy = pltpu.make_async_copy(pre_hbm, pre_ref, in_sems.at[1])
    pre_copy.start()
    cot_copy.wait()
    for c in range(COLS):
        cols_ref[pl.ds(c * TOK, TOK), :] = cot_ref[:, pl.ds(c * LANES, LANES)]
    sent = []
    for s in range(GROUP):
        sent.append(pltpu.make_async_copy(cols_ref, out_hbm.at[s, pl.ds(0, D), :], out_sems.at[0, s]))
        sent[-1].start()
    pre_copy.wait()
    for j in range(FFH // LANES):
        cols = pl.ds(j * LANES, LANES)
        value = pre_ref[:, cols].astype(jnp.float32)
        gate = pre_ref[:, pl.ds(FFH + j * LANES, LANES)].astype(jnp.float32)
        hidden = value * (gate * cdf_of(gate))
        ht_ref[cols, :] = hidden.T.astype(jnp.bfloat16)
    for s in range(GROUP):
        rows = ht_ref.at[pl.ds(GROUP_ORDER[s] * OWN, OWN), :]
        sent.append(pltpu.make_async_copy(rows, out_hbm.at[s, pl.ds(D, OWN), :], out_sems.at[1, s]))
        sent[-1].start()
    for copy in sent:
        copy.wait()


def factors_kernel(pre_ref, act_ref, slope_ref):
    for j in range(FFH // LANES):
        cols = pl.ds(j * LANES, LANES)
        value = pre_ref[:, cols].astype(jnp.float32)
        gate = pre_ref[:, pl.ds(FFH + j * LANES, LANES)].astype(jnp.float32)
        cdf = cdf_of(gate)
        dens = jnp.exp(-0.5 * gate * gate) * (1.0 / math.sqrt(2.0 * math.pi))
        act_ref[:, cols] = gate * cdf
        slope_ref[:, cols] = value * (cdf + gate * dens)


def products_kernel(scale, at_ref, in_ref, w_ref, dh_hbm, keep_ref, give_ref, flat_ref, parts_ref, dh_ref, sem):
    cots = jnp.concatenate(
        [
            jnp.concatenate([in_ref[s, pl.ds(c * TOK, TOK), :] for c in range(COLS)], axis=1)
            for s in range(GROUP)
        ],
        axis=0,
    )
    dht = lax.dot_general(w_ref[...], cots, (((1,), (1,)), ((), ())), preferred_element_type=jnp.float32)
    for s in range(GROUP):
        dh_ref[GROUP_ORDER[s]] = dht[:, s * TOK : (s + 1) * TOK]
    dh_copy = pltpu.make_async_copy(dh_ref, dh_hbm, sem)
    dh_copy.start()
    ht = jnp.concatenate([in_ref[s, pl.ds(D, OWN), :] for s in range(GROUP)], axis=1)
    total = jnp.dot(ht, cots, preferred_element_type=jnp.float32) * scale
    for c in range(COLS):
        flat_ref[pl.ds(c, OWN, stride=COLS), :] = total[:, c * LANES : (c + 1) * LANES]
    flat_ref[pl.ds(OWN * COLS, ROWS), :] = jnp.zeros((ROWS, LANES), jnp.float32)
    for far in range(FAR):
        for near in range(NEAR):
            first = (far * NEAR + near) * PIECE // LANES
            parts_ref[near, FAR_ORDER.index(far)] = flat_ref[pl.ds(first, ROWS), :]
    core = lax.rem(at_ref[0], 2)
    for half in range(2):
        keep_ref[half] = parts_ref[half * 2 + core]
        give_ref[half] = parts_ref[half * 2 + 1 - core]
    dh_copy.wait()


def core_sum_kernel(at_ref, own_ref, got_ref, keep_ref, give_ref):
    half = lax.div(at_ref[0], 2)
    keep_ref[...] = own_ref[half] + got_ref[half]
    give_ref[...] = (own_ref[1 - half] + got_ref[1 - half]).astype(jnp.bfloat16)


def near_sum_kernel(_, own_ref, got_ref, out_ref):
    out_ref[...] = (own_ref[...] + got_ref[...].astype(jnp.float32)).astype(jnp.bfloat16)


def d_pre_kernel(dh_ref, act_ref, slope_ref, out_ref, done_ref):
    done_ref[...] = jnp.zeros_like(done_ref)
    for j in range(FFH // LANES):
        cols = pl.ds(j * LANES, LANES)
        dh = dh_ref[cols, :].T
        out_ref[:, cols] = (dh * act_ref[:, cols]).astype(jnp.bfloat16)
        out_ref[:, pl.ds(FFH + j * LANES, LANES)] = (dh * slope_ref[:, cols]).astype(jnp.bfloat16)


def far_sum_kernel(at_ref, got_ref, out_ref, line_ref):
    total = jnp.zeros((ROWS, LANES), jnp.float32)
    for far in range(FAR):
        total += got_ref[far].astype(jnp.float32)
    for row in range(ROWS):
        line_ref[:, pl.ds(row * LANES, LANES)] = total[row : row + 1, :]
    for near in range(NEAR):

        @pl.when(at_ref[0] == near)
        def _():
            out_ref[...] = line_ref[:, pl.ds(near * PIECE % LANES, PIECE)]


def call(kernel, out, *args, flops=0, scratch=(), raw=(), raw_out=False, vmem=16 << 20):
    outs = out if isinstance(out, tuple) else (out,)
    moved = sum(a.size * a.dtype.itemsize for a in args) + sum(o.size * o.dtype.itemsize for o in outs)
    first = ANY if raw_out else VMEM
    return pl.pallas_call(
        kernel,
        out_shape=out,
        in_specs=[ANY if i in raw else SMEM if a.dtype == jnp.int32 else VMEM for i, a in enumerate(args)],
        out_specs=(first,) + (VMEM,) * (len(outs) - 1) if isinstance(out, tuple) else first,
        compiler_params=pltpu.CompilerParams(vmem_limit_bytes=vmem),
        cost_estimate=pl.CostEstimate(flops=flops, bytes_accessed=moved, transcendentals=0),
        scratch_shapes=list(scratch),
    )(*args)


def body(pre_acts, cotangent, w_out):
    scale = 1.0 / math.sqrt(TOK * GROUP * NEAR * FAR)
    bf16, f32 = jnp.bfloat16, jnp.float32
    S = jax.ShapeDtypeStruct
    at = (lax.axis_index("xh") * 2 + lax.axis_index("c")).astype(jnp.int32).reshape(1)

    outgoing = call(
        outgoing_kernel, S((GROUP, D + OWN, TOK), bf16), at, pre_acts, cotangent,
        scratch=[
            pltpu.VMEM((TOK, 2 * FFH), bf16),
            pltpu.VMEM((TOK, D), bf16),
            pltpu.VMEM((D, LANES), bf16),
            pltpu.VMEM((FFH, TOK), bf16),
            pltpu.SemaphoreType.DMA((2,)),
            pltpu.SemaphoreType.DMA((2, GROUP)),
        ],
        raw=(1, 2),
        raw_out=True,
        vmem=60 << 20,
    )
    incoming = lax.all_to_all(outgoing, GROUP_AXES, 0, 0, axis_index_groups=[GROUP_ORDER])
    block = (FAR, ROWS, LANES)
    dh, keep, give = call(
        lambda *refs: products_kernel(scale, *refs),
        (S((GROUP, OWN, TOK), f32), S((2,) + block, f32), S((2,) + block, f32)),
        at, incoming, w_out,
        flops=4 * OWN * D * TOK * GROUP,
        scratch=[
            pltpu.VMEM((OWN * COLS + ROWS, LANES), f32),
            pltpu.VMEM((NEAR,) + block, f32),
            pltpu.VMEM((GROUP, OWN, TOK), f32),
            pltpu.SemaphoreType.DMA,
        ],
        raw_out=True,
    )
    dh = lax.all_to_all(dh, GROUP_AXES, 0, 0)
    got = lax.ppermute(give, "c", [(0, 1), (1, 0)])
    keep, give = call(core_sum_kernel, (S(block, f32), S(block, bf16)), at, keep, got)
    got = lax.ppermute(give, "xh", [(0, 1), (1, 0)])
    act, slope = call(factors_kernel, (S((TOK, FFH), f32),) * 2, pre_acts)
    d_pre, done = call(d_pre_kernel, (S((TOK, 2 * FFH), bf16), S((ROWS, LANES), f32)), dh.reshape(FFH, TOK), act, slope)
    summed = call(near_sum_kernel, S(block, bf16), done, keep, got)
    got = lax.all_to_all(summed, "z", 0, 0, axis_index_groups=[FAR_ORDER])
    d_w = call(
        far_sum_kernel, S((1, PIECE), f32), at, got, scratch=[pltpu.VMEM((1, ROWS * LANES), f32)]
    )
    return (d_pre, d_w)


def solution(mesh):
    fine = Mesh(mesh.devices.reshape(FAR, 2, 2, 4, 2), DP_AXES + GROUP_AXES)
    return jax.shard_map(
        body,
        mesh=fine,
        in_specs=(P(DP_AXES + GROUP_AXES, None), P(DP_AXES + GROUP_AXES, None), P(GROUP_AXES, None)),
        out_specs=(P(DP_AXES + GROUP_AXES, None), P(GROUP_AXES, DP_AXES)),
        check_vma=False,
    )
```

```python
import math

import jax
import jax.numpy as jnp
from jax import lax
from jax.experimental import pallas as pl
from jax.experimental.pallas import tpu as pltpu
from jax.sharding import Mesh, PartitionSpec as P


D = 640
FFH = 1280
OWN = 160
GROUP = 8
TOK = 128
LANES = 128
COLS = D // LANES
FAR = 32
NEAR = 4
PIECE = 800
ROWS = 8
GROUP_AXES = ("y", "xl")
NEAR_AXES = ("xh", "c")
FAR_AXES = ("z",)
FAR_ORDER = [(i + 16) % FAR for i in range(FAR)]
DP_AXES = FAR_AXES + NEAR_AXES
VMEM = pl.BlockSpec(memory_space=pltpu.VMEM)
SMEM = pl.BlockSpec(memory_space=pltpu.SMEM)


def cdf_of(gate):
    return 0.5 * (1.0 + lax.erf(gate * (1.0 / math.sqrt(2.0))))


def outgoing_kernel(_, pre_ref, cot_ref, out_ref, ht_ref):
    for c in range(COLS):
        block = cot_ref[:, pl.ds(c * LANES, LANES)]
        for s in range(GROUP):
            out_ref[s, pl.ds(c * TOK, TOK), :] = block
    for j in range(FFH // LANES):
        cols = pl.ds(j * LANES, LANES)
        value = pre_ref[:, cols].astype(jnp.float32)
        gate = pre_ref[:, pl.ds(FFH + j * LANES, LANES)].astype(jnp.float32)
        hidden = value * (gate * cdf_of(gate))
        ht_ref[cols, :] = hidden.T.astype(jnp.bfloat16)
    for s in range(GROUP):
        out_ref[s, pl.ds(D, OWN), :] = ht_ref[pl.ds(s * OWN, OWN), :]


def factors_kernel(pre_ref, act_ref, slope_ref, done_ref):
    done_ref[...] = jnp.zeros_like(done_ref)
    for j in range(FFH // LANES):
        cols = pl.ds(j * LANES, LANES)
        value = pre_ref[:, cols].astype(jnp.float32)
        gate = pre_ref[:, pl.ds(FFH + j * LANES, LANES)].astype(jnp.float32)
        cdf = cdf_of(gate)
        dens = jnp.exp(-0.5 * gate * gate) * (1.0 / math.sqrt(2.0 * math.pi))
        act_ref[:, cols] = gate * cdf
        slope_ref[:, cols] = value * (cdf + gate * dens)


def products_kernel(scale, at_ref, in_ref, w_ref, dh_ref, keep_ref, give_ref, flat_ref, parts_ref):
    cots = jnp.concatenate(
        [
            jnp.concatenate([in_ref[s, pl.ds(c * TOK, TOK), :] for c in range(COLS)], axis=1)
            for s in range(GROUP)
        ],
        axis=0,
    )
    dht = lax.dot_general(w_ref[...], cots, (((1,), (1,)), ((), ())), preferred_element_type=jnp.float32)
    for s in range(GROUP):
        dh_ref[s] = dht[:, s * TOK : (s + 1) * TOK]
    ht = jnp.concatenate([in_ref[s, pl.ds(D, OWN), :] for s in range(GROUP)], axis=1)
    total = jnp.dot(ht, cots, preferred_element_type=jnp.float32) * scale
    for c in range(COLS):
        flat_ref[pl.ds(c, OWN, stride=COLS), :] = total[:, c * LANES : (c + 1) * LANES]
    flat_ref[pl.ds(OWN * COLS, ROWS), :] = jnp.zeros((ROWS, LANES), jnp.float32)
    for far in range(FAR):
        for near in range(NEAR):
            first = (far * NEAR + near) * PIECE // LANES
            parts_ref[near, FAR_ORDER.index(far)] = flat_ref[pl.ds(first, ROWS), :]
    core = lax.rem(at_ref[0], 2)
    for half in range(2):
        keep_ref[half] = parts_ref[half * 2 + core]
        give_ref[half] = parts_ref[half * 2 + 1 - core]


def core_sum_kernel(at_ref, own_ref, got_ref, keep_ref, give_ref):
    half = lax.div(at_ref[0], 2)
    keep_ref[...] = own_ref[half] + got_ref[half]
    give_ref[...] = (own_ref[1 - half] + got_ref[1 - half]).astype(jnp.bfloat16)


def near_sum_kernel(_, own_ref, got_ref, out_ref):
    out_ref[...] = (own_ref[...] + got_ref[...].astype(jnp.float32)).astype(jnp.bfloat16)


def last_kernel(at_ref, got_ref, dh_ref, act_ref, slope_ref, d_pre_ref, d_w_ref, line_ref):
    d_pre_part(dh_ref, act_ref, slope_ref, d_pre_ref)
    far_sum_part(at_ref, got_ref, d_w_ref, line_ref)


def d_pre_part(dh_ref, act_ref, slope_ref, out_ref):
    for j in range(FFH // LANES):
        cols = pl.ds(j * LANES, LANES)
        dh = dh_ref[cols, :].T
        out_ref[:, cols] = (dh * act_ref[:, cols]).astype(jnp.bfloat16)
        out_ref[:, pl.ds(FFH + j * LANES, LANES)] = (dh * slope_ref[:, cols]).astype(jnp.bfloat16)


def far_sum_part(at_ref, got_ref, out_ref, line_ref):
    total = jnp.zeros((ROWS, LANES), jnp.float32)
    for far in range(FAR):
        total += got_ref[far].astype(jnp.float32)
    for row in range(ROWS):
        line_ref[:, pl.ds(row * LANES, LANES)] = total[row : row + 1, :]
    for near in range(NEAR):

        @pl.when(at_ref[0] == near)
        def _():
            out_ref[...] = line_ref[:, pl.ds(near * PIECE % LANES, PIECE)]


def call(kernel, out, *args, flops=0, scratch=()):
    outs = out if isinstance(out, tuple) else (out,)
    moved = sum(a.size * a.dtype.itemsize for a in args) + sum(o.size * o.dtype.itemsize for o in outs)
    return pl.pallas_call(
        kernel,
        out_shape=out,
        in_specs=[SMEM if a.dtype == jnp.int32 else VMEM for a in args],
        out_specs=(VMEM,) * len(outs) if isinstance(out, tuple) else VMEM,
        compiler_params=pltpu.CompilerParams(vmem_limit_bytes=16 << 20),
        cost_estimate=pl.CostEstimate(flops=flops, bytes_accessed=moved, transcendentals=0),
        scratch_shapes=list(scratch),
    )(*args)


def body(pre_acts, cotangent, w_out):
    scale = 1.0 / math.sqrt(TOK * GROUP * NEAR * FAR)
    bf16, f32 = jnp.bfloat16, jnp.float32
    S = jax.ShapeDtypeStruct
    at = (lax.axis_index("xh") * 2 + lax.axis_index("c")).astype(jnp.int32).reshape(1)

    outgoing = call(
        outgoing_kernel, S((GROUP, D + OWN, TOK), bf16), at, pltpu.with_memory_space_constraint(pre_acts, pltpu.HBM), pltpu.with_memory_space_constraint(cotangent, pltpu.HBM),
        scratch=[pltpu.VMEM((FFH, TOK), bf16)],
    )
    incoming = lax.all_to_all(outgoing, GROUP_AXES, 0, 0)
    block = (FAR, ROWS, LANES)
    dh, keep, give = call(
        lambda *refs: products_kernel(scale, *refs),
        (S((GROUP, OWN, TOK), f32), S((2,) + block, f32), S((2,) + block, f32)),
        at, incoming, w_out,
        flops=4 * OWN * D * TOK * GROUP,
        scratch=[pltpu.VMEM((OWN * COLS + ROWS, LANES), f32), pltpu.VMEM((NEAR,) + block, f32)],
    )
    dh = lax.all_to_all(dh, GROUP_AXES, 0, 0)
    got = lax.ppermute(give, "c", [(0, 1), (1, 0)])
    keep, give = call(core_sum_kernel, (S(block, f32), S(block, bf16)), at, keep, got)
    got = lax.ppermute(give, "xh", [(0, 1), (1, 0)])
    act, slope, done = call(factors_kernel, (S((TOK, FFH), f32), S((TOK, FFH), f32), S((ROWS, LANES), f32)), pre_acts)
    summed = call(near_sum_kernel, S(block, bf16), done, keep, got)
    got = lax.all_to_all(summed, "z", 0, 0, axis_index_groups=[FAR_ORDER])
    d_pre, d_w = call(
        last_kernel, (S((TOK, 2 * FFH), bf16), S((1, PIECE), f32)), at, got, dh.reshape(FFH, TOK), act, slope,
        scratch=[pltpu.VMEM((1, ROWS * LANES), f32)],
    )
    return (d_pre, d_w)


def solution(mesh):
    fine = Mesh(mesh.devices.reshape(FAR, 2, 2, 4, 2), DP_AXES + GROUP_AXES)
    return jax.shard_map(
        body,
        mesh=fine,
        in_specs=(P(DP_AXES + GROUP_AXES, None), P(DP_AXES + GROUP_AXES, None), P(GROUP_AXES, None)),
        out_specs=(P(DP_AXES + GROUP_AXES, None), P(GROUP_AXES, DP_AXES)),
        check_vma=False,
    )
```

```python
import math

import jax
import jax.numpy as jnp
from jax import lax
from jax.experimental import pallas as pl
from jax.experimental.pallas import tpu as pltpu
from jax.sharding import Mesh, PartitionSpec as P


D = 640
FFH = 1280
OWN = 160
GROUP = 8
TOK = 128
LANES = 128
COLS = D // LANES
FAR = 32
NEAR = 4
PIECE = 800
ROWS = 8
GROUP_AXES = ("y", "xl")
NEAR_AXES = ("xh", "c")
FAR_AXES = ("z",)
GROUP_ORDER = [i ^ 5 for i in range(GROUP)]
FAR_ORDER = [(i + 16) % FAR for i in range(FAR)]
DP_AXES = FAR_AXES + NEAR_AXES
VMEM = pl.BlockSpec(memory_space=pltpu.VMEM)
SMEM = pl.BlockSpec(memory_space=pltpu.SMEM)


def cdf_of(gate):
    return 0.5 * (1.0 + lax.erf(gate * (1.0 / math.sqrt(2.0))))


def outgoing_kernel(_, pre_ref, cot_ref, out_ref, ht_ref):
    for c in range(COLS):
        block = cot_ref[:, pl.ds(c * LANES, LANES)]
        for s in range(GROUP):
            out_ref[s, pl.ds(c * TOK, TOK), :] = block
    for j in range(FFH // LANES):
        cols = pl.ds(j * LANES, LANES)
        value = pre_ref[:, cols].astype(jnp.float32)
        gate = pre_ref[:, pl.ds(FFH + j * LANES, LANES)].astype(jnp.float32)
        hidden = value * (gate * cdf_of(gate))
        ht_ref[cols, :] = hidden.T.astype(jnp.bfloat16)
    for s in range(GROUP):
        out_ref[s, pl.ds(D, OWN), :] = ht_ref[pl.ds(GROUP_ORDER[s] * OWN, OWN), :]


def factors_kernel(pre_ref, act_ref, slope_ref, done_ref):
    done_ref[...] = jnp.zeros_like(done_ref)
    for j in range(FFH // LANES):
        cols = pl.ds(j * LANES, LANES)
        value = pre_ref[:, cols].astype(jnp.float32)
        gate = pre_ref[:, pl.ds(FFH + j * LANES, LANES)].astype(jnp.float32)
        cdf = cdf_of(gate)
        dens = jnp.exp(-0.5 * gate * gate) * (1.0 / math.sqrt(2.0 * math.pi))
        act_ref[:, cols] = gate * cdf
        slope_ref[:, cols] = value * (cdf + gate * dens)


def products_kernel(scale, at_ref, in_ref, w_ref, dh_ref, keep_ref, give_ref, flat_ref, parts_ref):
    cots = jnp.concatenate(
        [
            jnp.concatenate([in_ref[s, pl.ds(c * TOK, TOK), :] for c in range(COLS)], axis=1)
            for s in range(GROUP)
        ],
        axis=0,
    )
    dht = lax.dot_general(w_ref[...], cots, (((1,), (1,)), ((), ())), preferred_element_type=jnp.float32)
    for s in range(GROUP):
        dh_ref[s] = dht[:, s * TOK : (s + 1) * TOK]
    ht = jnp.concatenate([in_ref[s, pl.ds(D, OWN), :] for s in range(GROUP)], axis=1)
    total = jnp.dot(ht, cots, preferred_element_type=jnp.float32) * scale
    for c in range(COLS):
        flat_ref[pl.ds(c, OWN, stride=COLS), :] = total[:, c * LANES : (c + 1) * LANES]
    flat_ref[pl.ds(OWN * COLS, ROWS), :] = jnp.zeros((ROWS, LANES), jnp.float32)
    for far in range(FAR):
        for near in range(NEAR):
            first = (far * NEAR + near) * PIECE // LANES
            parts_ref[near, FAR_ORDER.index(far)] = flat_ref[pl.ds(first, ROWS), :]
    core = lax.rem(at_ref[0], 2)
    for half in range(2):
        keep_ref[half] = parts_ref[half * 2 + core]
        give_ref[half] = parts_ref[half * 2 + 1 - core]


def core_sum_kernel(at_ref, own_ref, got_ref, keep_ref, give_ref):
    half = lax.div(at_ref[0], 2)
    keep_ref[...] = own_ref[half] + got_ref[half]
    give_ref[...] = (own_ref[1 - half] + got_ref[1 - half]).astype(jnp.bfloat16)


def near_sum_kernel(_, own_ref, got_ref, out_ref):
    out_ref[...] = (own_ref[...] + got_ref[...].astype(jnp.float32)).astype(jnp.bfloat16)


def last_kernel(at_ref, got_ref, dh_ref, act_ref, slope_ref, d_pre_ref, d_w_ref, line_ref):
    d_pre_part(dh_ref, act_ref, slope_ref, d_pre_ref)
    far_sum_part(at_ref, got_ref, d_w_ref, line_ref)


def d_pre_part(dh_ref, act_ref, slope_ref, out_ref):
    for j in range(FFH // LANES):
        cols = pl.ds(j * LANES, LANES)
        units = range(j * LANES, (j + 1) * LANES, 32)
        rows = [GROUP_ORDER.index(unit // OWN) * OWN + unit % OWN for unit in units]
        dh = jnp.concatenate([dh_ref[pl.ds(row, 32), :] for row in rows], axis=0).T
        out_ref[:, cols] = (dh * act_ref[:, cols]).astype(jnp.bfloat16)
        out_ref[:, pl.ds(FFH + j * LANES, LANES)] = (dh * slope_ref[:, cols]).astype(jnp.bfloat16)


def far_sum_part(at_ref, got_ref, out_ref, line_ref):
    total = jnp.zeros((ROWS, LANES), jnp.float32)
    for far in range(FAR):
        total += got_ref[far].astype(jnp.float32)
    for row in range(ROWS):
        line_ref[:, pl.ds(row * LANES, LANES)] = total[row : row + 1, :]
    for near in range(NEAR):

        @pl.when(at_ref[0] == near)
        def _():
            out_ref[...] = line_ref[:, pl.ds(near * PIECE % LANES, PIECE)]


def call(kernel, out, *args, flops=0, scratch=()):
    outs = out if isinstance(out, tuple) else (out,)
    moved = sum(a.size * a.dtype.itemsize for a in args) + sum(o.size * o.dtype.itemsize for o in outs)
    return pl.pallas_call(
        kernel,
        out_shape=out,
        in_specs=[SMEM if a.dtype == jnp.int32 else VMEM for a in args],
        out_specs=(VMEM,) * len(outs) if isinstance(out, tuple) else VMEM,
        compiler_params=pltpu.CompilerParams(vmem_limit_bytes=16 << 20),
        cost_estimate=pl.CostEstimate(flops=flops, bytes_accessed=moved, transcendentals=0),
        scratch_shapes=list(scratch),
    )(*args)


def body(pre_acts, cotangent, w_out):
    scale = 1.0 / math.sqrt(TOK * GROUP * NEAR * FAR)
    bf16, f32 = jnp.bfloat16, jnp.float32
    S = jax.ShapeDtypeStruct
    at = (lax.axis_index("xh") * 2 + lax.axis_index("c")).astype(jnp.int32).reshape(1)

    outgoing = call(
        outgoing_kernel, S((GROUP, D + OWN, TOK), bf16), at, pltpu.with_memory_space_constraint(pre_acts, pltpu.HBM), pltpu.with_memory_space_constraint(cotangent, pltpu.HBM),
        scratch=[pltpu.VMEM((FFH, TOK), bf16)],
    )
    incoming = lax.all_to_all(outgoing, GROUP_AXES, 0, 0, axis_index_groups=[GROUP_ORDER])
    block = (FAR, ROWS, LANES)
    dh, keep, give = call(
        lambda *refs: products_kernel(scale, *refs),
        (S((GROUP, OWN, TOK), f32), S((2,) + block, f32), S((2,) + block, f32)),
        at, incoming, w_out,
        flops=4 * OWN * D * TOK * GROUP,
        scratch=[pltpu.VMEM((OWN * COLS + ROWS, LANES), f32), pltpu.VMEM((NEAR,) + block, f32)],
    )
    dh = lax.all_to_all(dh, GROUP_AXES, 0, 0, axis_index_groups=[GROUP_ORDER])
    got = lax.ppermute(give, "c", [(0, 1), (1, 0)])
    keep, give = call(core_sum_kernel, (S(block, f32), S(block, bf16)), at, keep, got)
    got = lax.ppermute(give, "xh", [(0, 1), (1, 0)])
    act, slope, done = call(factors_kernel, (S((TOK, FFH), f32), S((TOK, FFH), f32), S((ROWS, LANES), f32)), pre_acts)
    summed = call(near_sum_kernel, S(block, bf16), done, keep, got)
    got = lax.all_to_all(summed, "z", 0, 0, axis_index_groups=[FAR_ORDER])
    d_pre, d_w = call(
        last_kernel, (S((TOK, 2 * FFH), bf16), S((1, PIECE), f32)), at, got, dh.reshape(FFH, TOK), act, slope,
        scratch=[pltpu.VMEM((1, ROWS * LANES), f32)],
    )
    return (d_pre, d_w)


def solution(mesh):
    fine = Mesh(mesh.devices.reshape(FAR, 2, 2, 4, 2), DP_AXES + GROUP_AXES)
    return jax.shard_map(
        body,
        mesh=fine,
        in_specs=(P(DP_AXES + GROUP_AXES, None), P(DP_AXES + GROUP_AXES, None), P(GROUP_AXES, None)),
        out_specs=(P(DP_AXES + GROUP_AXES, None), P(GROUP_AXES, DP_AXES)),
        check_vma=False,
    )
```
